32 devices in a mesh: fsdp: 4 (over y, x), tp: 8 (over z, core).
Axes of the slice: x: 2, y: 2, z: 4, core: 2. Of those that a mesh axis runs over, the one named last changes fastest.
Arguments:
- merged_weight: bfloat16 [4, 8192, 10240], P(None, ('fsdp', 'tp')), may hold values from -0.0625 to 0.0625
- hidden: bfloat16 [4, 1280, 8192], P('fsdp', None, 'tp'), may hold values from -6 to 6
- group_table: int32 [8], replicated, may hold values from 0 to 7, each once
Outputs:
- query: bfloat16 [4, 1280, 8192], P('fsdp', None, 'tp')
- keyvalue: bfloat16 [4, 1280, 2048], P('fsdp', None, 'tp')
The draws below stay inside these ranges and needn't reach their ends.
Inputs may be any that keep to these rules, and one draw needn't show every extreme that they name: `group_table`: every head group 0 .. 8 - 1 appears exactly once.
All inputs are finite; a program needn't handle non-finite values.
Results may differ from the reference program's by a relative error of at most 0.001.
Values may be sent and summed in bfloat16 or wider, within the bound.
A program may use at most 128 MiB of HBM per device.

```python
import jax
import jax.numpy as jnp
import numpy as np

D = 8192
Q_HEADS = 64
KV_HEADS = 8
HEAD_DIM = 128
TOKS = 1280
LAYERS = 4
COLS = 10240
N_TP = 8


def steps_of(own_key, dims, cuts, least, largest):
    level, own = 1.0, jax.random.fold_in(own_key, 6)
    for axis_at, parts in cuts:
        draws = jnp.exp(jax.random.uniform(jax.random.fold_in(own, axis_at), (parts,), jnp.float32, least / len(cuts), largest / len(cuts)))
        level = level * jnp.repeat(draws, dims[axis_at] // parts).reshape([-1 if axis == axis_at else 1 for axis in range(len(dims))])
    return level


def gaussian(own_key, shape, deviation, bound, cuts=(), kind=jnp.bfloat16):
    entries = jax.random.normal(own_key, shape, jnp.float32) * deviation
    if len(cuts) > 0:
        entries = steps_of(own_key, shape, cuts, -0.22, 0.18) * entries
    return jnp.clip(entries, min=-bound, max=bound).astype(kind)


def setup_inputs(seed: int = 0) -> dict:
    key_list = jax.random.split(jax.random.key(seed), 4)
    return {
        "merged_weight": gaussian(key_list[0], (LAYERS, D, COLS), D ** -0.5, 0.0625, ((1, 32),)),
        "hidden": gaussian(key_list[1], (LAYERS, TOKS, D), 1.0, 6.0, ((0, 4), (2, 8))),
        "group_table": jax.random.permutation(key_list[2], N_TP).astype(jnp.int32),
    }


def kv_heads_table(groups):
    per_group = max(KV_HEADS // groups, 1)
    table = np.zeros((groups, per_group), np.int32)
    for group in range(groups):
        for inner in range(per_group):
            table[group, inner] = (group * per_group + inner) * KV_HEADS // (groups * per_group)
    return table


def reference(merged_weight, hidden, group_table):
    query_list = []
    kv_list = []
    split = Q_HEADS * HEAD_DIM
    heads = jnp.asarray(kv_heads_table(N_TP).reshape(-1), dtype=jnp.int32)
    for layer in range(LAYERS):
        product = jnp.dot(hidden[layer], merged_weight[layer], preferred_element_type=jnp.float32).astype(jnp.bfloat16)
        q_part = product[:, :split].reshape(TOKS, N_TP, -1)
        kv_part = product[:, split:].reshape(TOKS, 2, KV_HEADS, HEAD_DIM)
        kv_part = kv_part.transpose(0, 2, 1, 3)
        kv_part = jnp.take(kv_part, heads, axis=1).reshape(TOKS, N_TP, -1)
        query_list.append(jnp.take(q_part, group_table, axis=1).reshape(TOKS, -1))
        kv_list.append(jnp.take(kv_part, group_table, axis=1).reshape(TOKS, -1))
    return jnp.stack(query_list), jnp.stack(kv_list)
```

```python
import functools

import jax
import jax.numpy as jnp
import numpy as np
from jax import lax
from jax.sharding import PartitionSpec as P

Q_HEADS = 64
KV_HEADS = 8
HEAD_DIM = 128
CORES = 2
AXES = ("fsdp", "tp")
TOP = 255.0


def unit_tables(chips):
    order = np.zeros((chips, chips), np.int32)
    for c in range(chips):
        order[c] = sorted(range(chips), key=lambda d: (-abs(d - c), -d))
    return order


def pick(blocks, table, c):
    named = sorted(set(int(v) for v in table if v >= 0))
    which = jnp.asarray(np.maximum(table, named[0]))[c]
    out = blocks[named[0]]
    for u in named[1:]:
        out = jnp.where(which == u, blocks[u], out)
    return out


def code(value, bound):
    scaled = value * (TOP / bound)
    return (scaled * jnp.abs(scaled)).astype(jnp.float16)


def decode(coded, bound):
    wide = coded.astype(jnp.float32)
    root = jnp.sqrt(jnp.abs(wide)) * (bound / TOP)
    return jnp.where(wide < 0, -root, root)


def shards(n_fsdp, n_tp, merged_weight, hidden, group_table):
    chips = n_tp // CORES
    half = chips // CORES
    layers, rows, _ = merged_weight.shape
    _, tokens, feats = hidden.shape
    part = feats // half
    assert layers == n_fsdp == chips and part == CORES * rows
    f = lax.axis_index("fsdp")
    t = lax.axis_index("tp")
    c, k = t // CORES, t % CORES

    def pairs(move):
        out = []
        for f0 in range(n_fsdp):
            for t0 in range(n_tp):
                to = move(f0, t0 // CORES, t0 % CORES)
                if to is not None:
                    f1, c1, k1 = to
                    out.append((f0 * n_tp + t0, f1 * n_tp + c1 * CORES + k1))
        return out

    def send(value, move):
        return lax.ppermute(value, AXES, pairs(move))

    def feature_move(delta):
        def move(f0, c0, k0):
            c1 = c0 + delta
            return (f0, c1, k0) if 0 <= c1 < chips and c1 // half == k0 else None
        return move

    pieces = []
    for delta in range(chips - 1, -chips, -1):
        at = jnp.remainder(c + delta + chips, half) * part
        piece = lax.dynamic_slice(hidden[0], (0, at), (tokens, part))
        pieces.append(piece if delta == 0 else send(piece, feature_move(delta)))
    mine = lax.dynamic_slice(jnp.stack(pieces), (chips - 1 - c, 0, 0), (chips, tokens, part))
    other = send(mine, lambda f0, c0, k0: (f0, c0, 1 - k0))
    mine = jnp.where(k == c // half, mine, other)
    feature_list = []
    for j in range(n_fsdp):
        for flip in range(CORES):
            feature_list.append(
                lax.dynamic_slice(
                    mine, (f ^ j, 0, (k ^ flip) * rows), (1, tokens, rows)
                )[0]
            )
    features = jnp.concatenate(feature_list, axis=1)

    q_width = Q_HEADS * HEAD_DIM // n_tp
    per_group = max(KV_HEADS // n_tp, 1)

    def columns(layer, slot):
        group = group_table[slot]
        take = lambda at, width: lax.dynamic_slice(
            merged_weight, (layer, 0, at), (1, rows, width)
        )[0]
        out = [take(group * q_width, q_width)]
        for inner in range(per_group):
            head = (group * per_group + inner) * KV_HEADS // (n_tp * per_group)
            for base in (Q_HEADS, Q_HEADS + KV_HEADS):
                out.append(take((base + head) * HEAD_DIM, HEAD_DIM))
        return jnp.concatenate(out, axis=1)

    order = unit_tables(chips)
    products, bounds = [], []
    for u in range(chips):
        d = jnp.asarray(order[:, u])[c]
        blocks = []
        for j in range(n_fsdp):
            for flip in range(CORES):
                block = columns(f ^ j, d * CORES + (k ^ flip))
                if j or flip:
                    block = send(
                        block, lambda f0, c0, k0: (f0 ^ j, c0, k0 ^ flip)
                    )
                blocks.append(block)
        weight = jnp.concatenate(blocks, axis=0)
        product = jnp.dot(features, weight, preferred_element_type=jnp.float32)
        products.append(product)
        bounds.append(jnp.max(jnp.abs(product)))

    where_is = np.zeros((chips, chips), np.int32)
    for c0 in range(chips):
        where_is[c0, order[c0]] = np.arange(chips)
    arrived = {}
    tiny = jnp.float32(1e-30)
    for step in range(chips - 1):
        reach = chips - 1 - step
        for way in (1, -1):
            table = np.array([
                where_is[c0, c0 + way * reach] if 0 <= c0 + way * reach < chips else -1
                for c0 in range(chips)
            ])
            total = pick(products, table, c)
            bound = pick(bounds, table, c) + tiny
            if step > 0:
                value, more = arrived[way]
                total, bound = total + value, bound + more
            move = lambda f0, c0, k0: (
                (f0, c0 + way, k0) if table[c0] >= 0 else None
            )
            coded = send(code(total, bound), move)
            more = send(jnp.full((8, 128), bound), move)[0, 0]
            arrived[way] = (decode(coded, more), more)
    result = products[chips - 1] + arrived[1][0] + arrived[-1][0]
    result = result.astype(jnp.bfloat16)[None]
    return result[:, :, :q_width], result[:, :, q_width:]


def solution(mesh):
    body = functools.partial(shards, mesh.shape["fsdp"], mesh.shape["tp"])
    return jax.shard_map(
        body,
        mesh=mesh,
        in_specs=(P(None, ("fsdp", "tp"), None), P("fsdp", None, "tp"), P()),
        out_specs=(P("fsdp", None, "tp"), P("fsdp", None, "tp")),
        check_vma=False,
    )
```

```python
import functools

import jax
import jax.numpy as jnp
import numpy as np
from jax import lax
from jax.experimental import pallas as pl
from jax.experimental.pallas import tpu as pltpu
from jax.sharding import PartitionSpec as P


Q_HEADS = 64
KV_HEADS = 8
HEAD_DIM = 128
CORES = 2
AXES = ("fsdp", "tp")
TOP = 255.0

TAIL = 16
PARTS = 2


def unit_tables(chips):
    order = np.zeros((chips, chips), np.int32)
    for c in range(chips):
        order[c] = sorted(range(chips), key=lambda d: (-abs(d - c), -d))
    return order


def pick(blocks, table, c):
    named = sorted(set(int(v) for v in table if v >= 0))
    which = jnp.asarray(np.maximum(table, named[0]))[c]
    out = blocks[named[0]]
    for u in named[1:]:
        out = jnp.where(which == u, blocks[u], out)
    return out


def code(value, bound):
    power = jnp.ceil(jnp.log2(bound))
    scaled = value * (TOP * jnp.exp2(-power))
    coded = (scaled * jnp.abs(scaled)).astype(jnp.float16)
    tail = jnp.full((TAIL, value.shape[1]), power).astype(jnp.float16)
    return jnp.concatenate([coded, tail], axis=0)


def decode(coded):
    bound = jnp.exp2(coded[-1, 0].astype(jnp.float32))
    wide = coded[:-TAIL].astype(jnp.float32)
    root = jnp.sqrt(jnp.abs(wide)) * (bound / TOP)
    return jnp.where(wide < 0, -root, root), bound


def select_kernel(pieces, table_ref, *refs):
    ins, outs = refs[: 3 * pieces], refs[3 * pieces :]
    for i in range(pieces):
        at = 0
        for part in ins[3 * i : 3 * i + 3]:
            width = part.shape[2]
            outs[i][:, at : at + width] = part[0]
            at += width


def select(table, merged_weight, q_width):
    pieces = table.shape[0]
    rows = merged_weight.shape[1]
    tile = max(rows // 4, 16)
    ins, outs = [], []
    width = q_width + 2 * HEAD_DIM
    for i in range(pieces):
        ins.append(pl.BlockSpec((1, tile, q_width), lambda r, s, i=i: (s[i, 0], r, s[i, 1])))
        for base in (Q_HEADS, Q_HEADS + KV_HEADS):
            ins.append(pl.BlockSpec(
                (1, tile, HEAD_DIM), lambda r, s, i=i, base=base: (s[i, 0], r, base + s[i, 2])
            ))
        outs.append(pl.BlockSpec((tile, width), lambda r, s: (r, 0)))
    return pl.pallas_call(
        functools.partial(select_kernel, pieces),
        grid_spec=pltpu.PrefetchScalarGridSpec(
            num_scalar_prefetch=1, grid=(rows // tile,), in_specs=ins, out_specs=outs
        ),
        out_shape=[jax.ShapeDtypeStruct((rows, width), merged_weight.dtype)] * pieces,
        cost_estimate=pl.CostEstimate(
            flops=0, bytes_accessed=4 * pieces * rows * width, transcendentals=0
        ),
    )(table, *([merged_weight] * (3 * pieces)))


def product_kernel(pieces, table_ref, *refs):
    features, weights = refs[:pieces], refs[pieces : 2 * pieces]
    out_ref, top_ref = refs[2 * pieces :]
    total = jnp.dot(features[0][0], weights[0][...], preferred_element_type=jnp.float32)
    for i in range(1, pieces):
        total += jnp.dot(features[i][0], weights[i][...], preferred_element_type=jnp.float32)
    out_ref[...] = total
    top = jnp.full(top_ref.shape, jnp.max(jnp.abs(total)))

    @pl.when(pl.program_id(0) == 0)
    def _():
        top_ref[...] = top

    @pl.when(pl.program_id(0) > 0)
    def _():
        top_ref[...] = jnp.maximum(top_ref[...], top)


def product(table, features, weights, first, tokens):
    pieces = len(weights)
    rows, width = weights[0].shape
    tile = 128
    start = first // tile
    ins = [
        pl.BlockSpec((1, tile, rows), lambda r, s, i=i: (s[i, 0], start + r, s[i, 1]))
        for i in range(pieces)
    ]
    ins += [pl.BlockSpec((rows, width), lambda r, s: (0, 0))] * pieces
    out, top = pl.pallas_call(
        functools.partial(product_kernel, pieces),
        grid_spec=pltpu.PrefetchScalarGridSpec(
            num_scalar_prefetch=1,
            grid=(tokens // tile,),
            in_specs=ins,
            out_specs=[
                pl.BlockSpec((tile, width), lambda r, s: (r, 0)),
                pl.BlockSpec((8, 128), lambda r, s: (0, 0)),
            ],
        ),
        out_shape=[
            jax.ShapeDtypeStruct((tokens, width), jnp.float32),
            jax.ShapeDtypeStruct((8, 128), jnp.float32),
        ],
        cost_estimate=pl.CostEstimate(
            flops=2 * tokens * pieces * rows * width,
            bytes_accessed=2 * pieces * rows * (width + tokens) + 4 * tokens * width,
            transcendentals=0,
        ),
    )(table, *([features] * pieces), *weights)
    return out, top[0, 0]


def shards(n_fsdp, n_tp, merged_weight, hidden, group_table):
    chips = n_tp // CORES
    half = chips // CORES
    layers, rows, _ = merged_weight.shape
    _, tokens, feats = hidden.shape
    part = feats // half
    assert layers == n_fsdp == chips and part == CORES * rows
    f = lax.axis_index("fsdp")
    t = lax.axis_index("tp")
    c, k = t // CORES, t % CORES

    def pairs(move):
        out = []
        for f0 in range(n_fsdp):
            for t0 in range(n_tp):
                to = move(f0, t0 // CORES, t0 % CORES)
                if to is not None:
                    f1, c1, k1 = to
                    out.append((f0 * n_tp + t0, f1 * n_tp + c1 * CORES + k1))
        return out

    def send(value, move):
        return lax.ppermute(value, AXES, pairs(move))

    def feature_move(delta):
        def move(f0, c0, k0):
            c1 = c0 + delta
            return (f0, c1, k0) if 0 <= c1 < chips and c1 // half == k0 else None

        return move

    pieces = {}
    for delta in range(chips - 1, -chips, -1):
        at = jnp.remainder(c + delta + chips, half) * part
        piece = lax.dynamic_slice(hidden[0], (0, at), (tokens, part))
        if delta:
            piece = send(piece, feature_move(delta))
        pieces[delta] = piece
    features = []
    for source in range(chips):
        table = np.arange(chips) - source
        near = pieces_of(pieces, table, c)
        far = send(near, lambda f0, c0, k0: (f0, c0, 1 - k0))
        features.append(jnp.where(k == c // half, near, far))
    features = jnp.stack(features)
    narrow = rows % 128 != 0
    if narrow:
        features = features.reshape(chips, tokens, CORES, rows).swapaxes(1, 2)
        features = features.reshape(chips * CORES, tokens, rows)

    q_width = Q_HEADS * HEAD_DIM // n_tp
    assert KV_HEADS <= n_tp
    order = unit_tables(chips)
    hops = np.array([(j, flip) for j in range(n_fsdp) for flip in range(CORES)], np.int32)
    layer = f ^ hops[:, 0]
    core = k ^ hops[:, 1]
    feature_table = jnp.stack(
        [layer * CORES + core, jnp.zeros_like(core)] if narrow else [layer, core], axis=1
    )
    group = group_table[(jnp.asarray(order)[c] * CORES)[:, None] + core[None, :]]
    columns = jnp.stack(
        [jnp.broadcast_to(layer, group.shape), group, group * KV_HEADS // n_tp], axis=2
    )
    arrived_weights = []
    for u in range(chips):
        blocks = select(columns[u], merged_weight, q_width)
        here = []
        for i, (j, flip) in enumerate(hops.tolist()):
            block = blocks[i]
            if i:
                block = send(block, lambda f0, c0, k0: (f0 ^ j, c0, k0 ^ flip))
            here.append(block)
        arrived_weights.append(here)
    count = tokens // PARTS
    products = [[None] * chips for _ in range(PARTS)]
    bounds = [[None] * chips for _ in range(PARTS)]
    for u in range(chips):
        for b in range(PARTS):
            products[b][u], bounds[b][u] = product(
                feature_table, features, arrived_weights[u], b * count, count
            )

    where_is = np.zeros((chips, chips), np.int32)
    for c0 in range(chips):
        where_is[c0, order[c0]] = np.arange(chips)
    arrived = {}
    tiny = jnp.float32(1e-30)
    for step in range(chips - 1):
        reach = chips - 1 - step
        for b in range(PARTS):
            for way in (1, -1):
                table = np.array([
                    where_is[c0, c0 + way * reach] if 0 <= c0 + way * reach < chips else -1
                    for c0 in range(chips)
                ])
                total = pick(products[b], table, c)
                bound = pick(bounds[b], table, c) + tiny
                if step > 0:
                    value, more = decode(arrived[way, b])
                    total, bound = total + value, bound + more
                move = lambda f0, c0, k0: (
                    (f0, c0 + way, k0) if table[c0] >= 0 else None
                )
                coded = code(total, bound)
                arrived[way, b] = send(coded, move)
    result = []
    for b in range(PARTS):
        total = products[b][chips - 1]
        for way in (1, -1):
            total = total + decode(arrived[way, b])[0]
        result.append(total.astype(jnp.bfloat16))
    result = jnp.concatenate(result, axis=0)[None]
    return result[:, :, :q_width], result[:, :, q_width:]


def pieces_of(pieces, table, c):
    out = None
    for c0, distance in enumerate(table.tolist()):
        piece = pieces[distance]
        out = piece if out is None else jnp.where(c == c0, piece, out)
    return out


def solution(mesh):
    n_fsdp, n_tp = mesh.shape["fsdp"], mesh.shape["tp"]

    def body(*args):
        return shards(n_fsdp, n_tp, *args)

    return jax.shard_map(
        body,
        mesh=mesh,
        in_specs=(P(None, ("fsdp", "tp"), None), P("fsdp", None, "tp"), P()),
        out_specs=(P("fsdp", None, "tp"), P("fsdp", None, "tp")),
        check_vma=False,
    )
```
